32 devices in a mesh: seq: 16 (over z, y, x), head: 2 (over core).
Axes of the slice: x: 2, y: 2, z: 4, core: 2. Of those that a mesh axis runs over, the one named last changes fastest.
Arguments:
- queries: bfloat16 [16384, 32, 128], P('seq', 'head'), may hold values from -6 to 6
- key_rows: bfloat16 [16384, 32, 128], P('seq', 'head'), may hold values from -6 to 6
- value_rows: bfloat16 [16384, 32, 128], P('seq', 'head'), may hold values from -6 to 6
- level_weights: float32 [7, 32, 16384], P(None, 'head', 'seq'), may hold values from 0.2 to 30
- out_gain: float32 [32, 128], P('head'), may hold values from 0.25 to 1.75
Outputs:
- attended: bfloat16 [16384, 32, 128], P('seq', 'head')
The draws below stay inside these ranges and needn't reach their ends.
All inputs are finite; a program needn't handle non-finite values.
Results may differ from the reference program's by a relative error of at most 0.0062.
Values may be sent and summed in bfloat16 or wider, within the bound.
A program may use at most 192 MiB of HBM per device.

```python
import math
import jax
import jax.numpy as jnp
from jax import lax

HEADS = 32
HEAD_DIM = 128
STRETCH = 256
TOK_DEV = 1024
TOKENS = 16384
LEVELS = 7


def draw_level_weights(key, part):
    shape = (LEVELS, HEADS, TOKENS)
    rising = jnp.arange(HEADS, dtype=jnp.float32) / (HEADS - 1)
    base = jnp.exp(jax.random.uniform(key, shape, jnp.float32, math.log(0.2), 0.0))
    factor = jnp.exp(rising * math.log(10.0))
    return base * factor[None, :, None]


def shard_levels(key, extent, cuts, low, top_value):
    gain, own = 1.0, jax.random.fold_in(key, 6)
    for dim, parts in cuts:
        heights = jnp.exp(jax.random.uniform(jax.random.fold_in(own, dim), (parts,), jnp.float32, low / len(cuts), top_value / len(cuts)))
        gain = gain * jnp.repeat(heights, extent[dim] // parts).reshape([-1 if axis == dim else 1 for axis in range(len(extent))])
    return gain


def centred(own_key, extent, width, limit, shards=(), kind=jnp.bfloat16):
    level = shard_levels(own_key, extent, shards, -0.22, 0.18) if shards else 1.0
    result = jax.random.normal(own_key, extent, jnp.float32) * width * level
    return jnp.minimum(jnp.maximum(result, -limit), limit).astype(kind)


def setup_inputs(seed: int = 0) -> dict:
    splits = jax.random.split(jax.random.key(seed), 6)
    return {
        "queries": centred(splits[0], (TOKENS, HEADS, HEAD_DIM), 1.0, 6.0, ((0, 16), (1, 2))),
        "key_rows": centred(splits[1], (TOKENS, HEADS, HEAD_DIM), 1.0, 6.0, ((0, 16), (1, 2))),
        "value_rows": centred(splits[2], (TOKENS, HEADS, HEAD_DIM), 1.0, 6.0, ((0, 16), (1, 2))),
        "level_weights": draw_level_weights(jax.random.fold_in(splits[5], 71), 0),
        "out_gain": jnp.clip(1.0 + 0.15 * jax.random.normal(splits[4], (HEADS, HEAD_DIM), jnp.float32), 0.25, 1.75),
    }


def head_mix(query_head, key_head, value_head, weight_head):
    per_seg = TOK_DEV // STRETCH
    block_count = TOKENS // STRETCH
    seg_count = TOKENS // TOK_DEV
    score_scale = 1.0 / math.sqrt(HEAD_DIM)
    query_blocks = query_head.astype(jnp.float32).reshape(block_count, STRETCH, HEAD_DIM)
    key_blocks = key_head.astype(jnp.float32).reshape(block_count, STRETCH, HEAD_DIM)
    value_blocks = value_head.astype(jnp.float32).reshape(block_count, STRETCH, HEAD_DIM)
    zero_block = jnp.zeros((1, STRETCH, HEAD_DIM), jnp.float32)
    prev_keys = jnp.concatenate([zero_block, key_blocks[:-1]], 0)
    prev_values = jnp.concatenate([zero_block, value_blocks[:-1]], 0)
    positions = jnp.arange(STRETCH)
    causal = positions[:, None] >= positions[None, :]
    own_scores = jnp.einsum('ntd,nud->ntu', query_blocks, key_blocks) * score_scale
    own_scores = jnp.where(causal[None], own_scores, 0.0).astype(jnp.bfloat16)
    prev_scores = (jnp.einsum('ntd,nud->ntu', query_blocks, prev_keys) * score_scale).astype(jnp.bfloat16)
    own_part = jnp.einsum('ntu,nud->ntd', own_scores.astype(jnp.float32), value_blocks)
    prev_part = jnp.einsum('ntu,nud->ntd', prev_scores.astype(jnp.float32), prev_values)
    block_states = jnp.einsum('nud,nue->nde', key_blocks, value_blocks)
    seg_rounded = lax.optimization_barrier(jnp.sum(block_states.reshape(seg_count, per_seg, HEAD_DIM, HEAD_DIM), 1)).astype(jnp.bfloat16)
    seg_totals = lax.optimization_barrier(seg_rounded).astype(jnp.float32)
    far_weights = weight_head[2:]

    def far_block(index):
        states = []
        last_state = lax.dynamic_index_in_dim(block_states, jnp.maximum(index - 1, 0).astype(jnp.int32), 0, keepdims=False)
        for level_bit in range(1, LEVELS - 1):
            span = 2 ** level_bit
            start = (index >> level_bit + 1 << level_bit + 1).astype(jnp.int32)
            present = (index >> level_bit & 1).astype(jnp.float32)
            lowest = present * (index & span - 1 == 0).astype(jnp.float32)
            if span < per_seg:
                total = lax.optimization_barrier(jnp.sum(lax.dynamic_slice_in_dim(block_states, start, span, 0), 0))
            else:
                total = lax.optimization_barrier(jnp.sum(lax.dynamic_slice_in_dim(seg_totals, (start // per_seg).astype(jnp.int32), span // per_seg, 0), 0))
            states.append(present * (total - lowest * last_state))
        stacked = lax.optimization_barrier(jnp.stack(states).astype(jnp.bfloat16)).astype(jnp.float32)
        rows = lax.dynamic_slice_in_dim(query_head, (index * STRETCH).astype(jnp.int32), STRETCH, 0).astype(jnp.float32)
        weights = lax.dynamic_slice_in_dim(far_weights, (index * STRETCH).astype(jnp.int32), STRETCH, 1)
        scaled = (rows[None, :, :] * weights[:, :, None] * score_scale).astype(jnp.bfloat16)
        scaled = lax.optimization_barrier(scaled).astype(jnp.float32)
        return jnp.einsum('ltd,lde->te', scaled, stacked)
    far_part = lax.map(far_block, jnp.arange(block_count, dtype=jnp.int32)).reshape(TOKENS, HEAD_DIM)
    own_flat = own_part.reshape(TOKENS, HEAD_DIM)
    prev_flat = prev_part.reshape(TOKENS, HEAD_DIM)
    return weight_head[0][:, None] * own_flat + weight_head[1][:, None] * prev_flat + far_part

def reference(queries, key_rows, value_rows, level_weights, out_gain):

    def one_head(packed):
        return head_mix(packed[0], packed[1], packed[2], packed[3])
    mixed_all = lax.map(one_head, (jnp.transpose(queries, (1, 0, 2)), jnp.transpose(key_rows, (1, 0, 2)), jnp.transpose(value_rows, (1, 0, 2)), jnp.transpose(level_weights, (1, 0, 2))))
    mean_square = lax.optimization_barrier(jnp.sum(mixed_all * mixed_all, axis=(0, 2))) / (HEADS * HEAD_DIM)
    normed = mixed_all * lax.rsqrt(mean_square + 1e-06)[None, :, None] * out_gain[:, None, :]
    return jnp.transpose(normed, (1, 0, 2)).astype(jnp.bfloat16)
```

```python
import math

import jax
import jax.numpy as jnp
import numpy as np
from jax import lax
from jax.sharding import PartitionSpec as P

HEADS = 32
HEAD_DIM = 128
STRETCH = 256


def shifted(x, axis, by):
    devices = lax.axis_size(axis)
    pairs = [(i, i + by) for i in range(devices) if 0 <= i + by < devices]
    return lax.ppermute(x, axis, pairs)


def on_device(queries, key_rows, value_rows, level_weights, out_gain):
    tok_count, head_count, head_width = queries.shape
    level_count = level_weights.shape[0]
    block_count = tok_count // STRETCH
    inner_bits = block_count.bit_length() - 1
    seq_bits = lax.axis_size("seq").bit_length() - 1
    seq_index = lax.axis_index("seq")
    score_scale = 1.0 / math.sqrt(head_width)
    query_blocks = queries.reshape(block_count, STRETCH, head_count, head_width)
    key_blocks = key_rows.reshape(block_count, STRETCH, head_count, head_width)
    value_blocks = value_rows.reshape(block_count, STRETCH, head_count, head_width)
    last_pair = jnp.stack([key_rows[tok_count - STRETCH :], value_rows[tok_count - STRETCH :]])
    arrived = shifted(last_pair, "seq", 1)
    halo_keys = arrived[0]
    halo_values = arrived[1]
    prev_keys = jnp.concatenate([halo_keys[None], key_blocks[:-1]], 0)
    prev_values = jnp.concatenate([halo_values[None], value_blocks[:-1]], 0)
    positions = jnp.arange(STRETCH)
    causal = positions[:, None] >= positions[None, :]
    own_scores = (
        jnp.einsum("cthd,cuhd->chtu", query_blocks, key_blocks, preferred_element_type=jnp.float32)
        * score_scale
    )
    own_scores = jnp.where(causal, own_scores, 0.0).astype(jnp.bfloat16)
    prev_scores = (
        jnp.einsum("cthd,cuhd->chtu", query_blocks, prev_keys, preferred_element_type=jnp.float32)
        * score_scale
    ).astype(jnp.bfloat16)
    own_part = jnp.einsum(
        "chtu,cuhd->cthd", own_scores, value_blocks, preferred_element_type=jnp.float32
    )
    prev_part = jnp.einsum(
        "chtu,cuhd->cthd", prev_scores, prev_values, preferred_element_type=jnp.float32
    )
    block_states = jnp.einsum(
        "cuhd,cuhe->chde", key_blocks, value_blocks, preferred_element_type=jnp.float32
    )
    halo_state = jnp.einsum(
        "uhd,uhe->hde", halo_keys, halo_values, preferred_element_type=jnp.float32
    )
    device_total = jnp.sum(block_states, 0).astype(jnp.bfloat16).astype(jnp.float32)
    seq_count = lax.axis_size("seq")
    group_rows = []
    running = device_total
    for level_bit in range(seq_bits):
        span = 1 << level_bit
        pairs = [(i, i ^ span) for i in range(seq_count)]
        partner = lax.ppermute(running, "seq", pairs)
        target_high = (seq_index >> level_bit & 1 == 1).astype(jnp.float32)
        group_rows.append(target_high * partner)
        if level_bit + 1 < seq_bits:
            running = running + partner
    group_sums = jnp.stack(group_rows)
    inner_rows = []
    for target in range(block_count):
        level_rows = []
        for level_bit in range(1, inner_bits):
            span = 1 << level_bit
            if target >> level_bit & 1:
                start = target >> level_bit + 1 << level_bit + 1
                total = block_states[start]
                for source in range(start + 1, start + span):
                    if source != target - 1:
                        total = total + block_states[source]
                level_rows.append(total)
            else:
                level_rows.append(jnp.zeros_like(block_states[0]))
        if level_rows:
            inner_rows.append(jnp.stack(level_rows))
    lowest_flags = jnp.stack(
        [
            ((seq_index >> level_bit & 1 == 1) & (seq_index & (1 << level_bit) - 1 == 0)).astype(
                jnp.float32
            )
            for level_bit in range(seq_bits)
        ]
    )
    first_block = (jnp.arange(block_count) == 0).astype(jnp.float32)
    correction = lowest_flags[:, None, None, None] * halo_state[None]
    outer_states = group_sums[None] - first_block[:, None, None, None, None] * correction[None]
    if inner_rows:
        inner_states = jnp.stack(inner_rows)
        outer_states = jnp.concatenate([inner_states, outer_states], 1)
    far_states = outer_states.astype(jnp.bfloat16)
    weight_blocks = jnp.transpose(
        level_weights.reshape(level_count, head_count, block_count, STRETCH), (2, 3, 1, 0)
    )
    scaled = (
        query_blocks[:, :, :, None, :] * weight_blocks[:, :, :, 2:, None] * score_scale
    ).astype(jnp.bfloat16)
    far_part = jnp.einsum(
        "cthld,clhde->cthe", scaled, far_states, preferred_element_type=jnp.float32
    )
    mixed_out = (
        weight_blocks[:, :, :, 0:1] * own_part + weight_blocks[:, :, :, 1:2] * prev_part + far_part
    )
    mixed_out = mixed_out.reshape(tok_count, head_count, head_width)
    square_sum = jnp.sum(mixed_out * mixed_out, axis=(1, 2))
    whole_sum = lax.psum(square_sum, "head")
    inverse = lax.rsqrt(whole_sum / (HEADS * HEAD_DIM) + 1e-06)
    return (mixed_out * inverse[:, None, None] * out_gain[None]).astype(jnp.bfloat16)


def solution(mesh):
    placed = (
        P("seq", "head", None),
        P("seq", "head", None),
        P("seq", "head", None),
        P(None, "head", "seq"),
        P("head", None),
    )
    return jax.shard_map(
        on_device, mesh=mesh, in_specs=placed, out_specs=P("seq", "head", None), check_vma=False
    )
```

```python
import math

import jax
import jax.numpy as jnp
import numpy as np
from jax import lax
from jax.sharding import PartitionSpec as P

HEADS = 32
HEAD_DIM = 128
STRETCH = 256


def shifted(x, axis, by):
    devices = lax.axis_size(axis)
    pairs = [(i, i + by) for i in range(devices) if 0 <= i + by < devices]
    return lax.ppermute(x, axis, pairs)


def on_device(queries, key_rows, value_rows, level_weights, out_gain):
    tok_count, head_count, head_width = queries.shape
    level_count = level_weights.shape[0]
    block_count = tok_count // STRETCH
    inner_bits = block_count.bit_length() - 1
    seq_bits = lax.axis_size("seq").bit_length() - 1
    seq_index = lax.axis_index("seq")
    score_scale = 1.0 / math.sqrt(head_width)
    query_blocks = queries.reshape(block_count, STRETCH, head_count, head_width)
    key_blocks = key_rows.reshape(block_count, STRETCH, head_count, head_width)
    value_blocks = value_rows.reshape(block_count, STRETCH, head_count, head_width)
    last_pair = jnp.stack([key_rows[tok_count - STRETCH :], value_rows[tok_count - STRETCH :]])
    arrived = shifted(last_pair, "seq", 1)
    halo_keys = arrived[0]
    halo_values = arrived[1]
    prev_keys = jnp.concatenate([halo_keys[None], key_blocks[:-1]], 0)
    prev_values = jnp.concatenate([halo_values[None], value_blocks[:-1]], 0)
    positions = jnp.arange(STRETCH)
    causal = positions[:, None] >= positions[None, :]
    own_scores = (
        jnp.einsum("cthd,cuhd->chtu", query_blocks, key_blocks, preferred_element_type=jnp.float32)
        * score_scale
    )
    own_scores = jnp.where(causal, own_scores, 0.0).astype(jnp.bfloat16)
    prev_scores = (
        jnp.einsum("cthd,cuhd->chtu", query_blocks, prev_keys, preferred_element_type=jnp.float32)
        * score_scale
    ).astype(jnp.bfloat16)
    own_part = jnp.einsum(
        "chtu,cuhd->cthd", own_scores, value_blocks, preferred_element_type=jnp.float32
    )
    prev_part = jnp.einsum(
        "chtu,cuhd->cthd", prev_scores, prev_values, preferred_element_type=jnp.float32
    )
    block_states = jnp.einsum(
        "cuhd,cuhe->chde", key_blocks, value_blocks, preferred_element_type=jnp.float32
    )
    halo_state = jnp.einsum(
        "uhd,uhe->hde", halo_keys, halo_values, preferred_element_type=jnp.float32
    )
    device_total = jnp.sum(block_states, 0).astype(jnp.bfloat16).astype(jnp.float32)
    seq_count = lax.axis_size("seq")
    group_rows = []
    running = device_total
    for level_bit in range(seq_bits):
        span = 1 << level_bit
        pairs = [(i, i ^ span) for i in range(seq_count)]
        if level_bit + 1 == seq_bits:
            pairs = [(i, i ^ span) for i in range(seq_count) if not i & span]
        partner = lax.ppermute(running.astype(jnp.bfloat16), "seq", pairs).astype(jnp.float32)
        target_high = (seq_index >> level_bit & 1 == 1).astype(jnp.float32)
        group_rows.append(target_high * partner)
        if level_bit + 1 < seq_bits:
            running = running + partner
    group_sums = jnp.stack(group_rows)
    inner_rows = []
    for target in range(block_count):
        level_rows = []
        for level_bit in range(1, inner_bits):
            span = 1 << level_bit
            if target >> level_bit & 1:
                start = target >> level_bit + 1 << level_bit + 1
                total = block_states[start]
                for source in range(start + 1, start + span):
                    if source != target - 1:
                        total = total + block_states[source]
                level_rows.append(total)
            else:
                level_rows.append(jnp.zeros_like(block_states[0]))
        if level_rows:
            inner_rows.append(jnp.stack(level_rows))
    lowest_flags = jnp.stack(
        [
            ((seq_index >> level_bit & 1 == 1) & (seq_index & (1 << level_bit) - 1 == 0)).astype(
                jnp.float32
            )
            for level_bit in range(seq_bits)
        ]
    )
    first_block = (jnp.arange(block_count) == 0).astype(jnp.float32)
    correction = lowest_flags[:, None, None, None] * halo_state[None]
    outer_states = group_sums[None] - first_block[:, None, None, None, None] * correction[None]
    if inner_rows:
        inner_states = jnp.stack(inner_rows)
        outer_states = jnp.concatenate([inner_states, outer_states], 1)
    far_states = outer_states.astype(jnp.bfloat16)
    weight_blocks = jnp.transpose(
        level_weights.reshape(level_count, head_count, block_count, STRETCH), (2, 3, 1, 0)
    )
    scaled = (
        query_blocks[:, :, :, None, :] * weight_blocks[:, :, :, 2:, None] * score_scale
    ).astype(jnp.bfloat16)
    far_part = jnp.einsum(
        "cthld,clhde->cthe", scaled, far_states, preferred_element_type=jnp.float32
    )
    mixed_out = (
        weight_blocks[:, :, :, 0:1] * own_part + weight_blocks[:, :, :, 1:2] * prev_part + far_part
    )
    mixed_out = mixed_out.reshape(tok_count, head_count, head_width)
    square_sum = jnp.sum(mixed_out * mixed_out, axis=(1, 2))
    whole_sum = lax.psum(square_sum, "head")
    inverse = lax.rsqrt(whole_sum / (HEADS * HEAD_DIM) + 1e-06)
    return (mixed_out * inverse[:, None, None] * out_gain[None]).astype(jnp.bfloat16)


def solution(mesh):
    placed = (
        P("seq", "head", None),
        P("seq", "head", None),
        P("seq", "head", None),
        P(None, "head", "seq"),
        P("head", None),
    )
    return jax.shard_map(
        on_device, mesh=mesh, in_specs=placed, out_specs=P("seq", "head", None), check_vma=False
    )
```

```python
import math

import jax
import jax.numpy as jnp
import numpy as np
from jax import lax
from jax.sharding import PartitionSpec as P

HEADS = 32
HEAD_DIM = 128
STRETCH = 256


def shifted(x, axis, by):
    devices = lax.axis_size(axis)
    pairs = [(i, i + by) for i in range(devices) if 0 <= i + by < devices]
    return lax.ppermute(x, axis, pairs)


def on_device(queries, key_rows, value_rows, level_weights, out_gain):
    tok_count, head_count, head_width = queries.shape
    level_count = level_weights.shape[0]
    block_count = tok_count // STRETCH
    inner_bits = block_count.bit_length() - 1
    seq_bits = lax.axis_size("seq").bit_length() - 1
    seq_index = lax.axis_index("seq")
    score_scale = 1.0 / math.sqrt(head_width)
    query_blocks = queries.reshape(block_count, STRETCH, head_count, head_width)
    key_blocks = key_rows.reshape(block_count, STRETCH, head_count, head_width)
    value_blocks = value_rows.reshape(block_count, STRETCH, head_count, head_width)
    last_pair = jnp.stack([key_rows[tok_count - STRETCH :], value_rows[tok_count - STRETCH :]])
    arrived = shifted(last_pair, "seq", 1)
    halo_keys = arrived[0]
    halo_values = arrived[1]
    prev_keys = jnp.concatenate([halo_keys[None], key_blocks[:-1]], 0)
    prev_values = jnp.concatenate([halo_values[None], value_blocks[:-1]], 0)
    positions = jnp.arange(STRETCH)
    causal = positions[:, None] >= positions[None, :]
    own_scores = (
        jnp.einsum("cthd,cuhd->chtu", query_blocks, key_blocks, preferred_element_type=jnp.float32)
        * score_scale
    )
    own_scores = jnp.where(causal, own_scores, 0.0).astype(jnp.bfloat16)
    prev_scores = (
        jnp.einsum("cthd,cuhd->chtu", query_blocks, prev_keys, preferred_element_type=jnp.float32)
        * score_scale
    ).astype(jnp.bfloat16)
    own_part = jnp.einsum(
        "chtu,cuhd->cthd", own_scores, value_blocks, preferred_element_type=jnp.float32
    )
    prev_part = jnp.einsum(
        "chtu,cuhd->cthd", prev_scores, prev_values, preferred_element_type=jnp.float32
    )
    block_states = jnp.einsum(
        "cuhd,cuhe->chde", key_blocks, value_blocks, preferred_element_type=jnp.float32
    )
    halo_state = jnp.einsum(
        "uhd,uhe->hde", halo_keys, halo_values, preferred_element_type=jnp.float32
    )
    device_total = jnp.sum(block_states, 0).astype(jnp.bfloat16).astype(jnp.float32)
    seq_count = lax.axis_size("seq")
    group_rows = []
    running = device_total
    for level_bit in range(seq_bits):
        span = 1 << level_bit
        pairs = [(i, i ^ span) for i in range(seq_count)]
        if level_bit + 1 == seq_bits:
            pairs = [(i, i ^ span) for i in range(seq_count) if not i & span]
        partner = lax.ppermute(running.astype(jnp.bfloat16), "seq", pairs).astype(jnp.float32)
        if level_bit == min(1, seq_bits - 1):
            partner, own_part, prev_part = lax.optimization_barrier((partner, own_part, prev_part))
        target_high = (seq_index >> level_bit & 1 == 1).astype(jnp.float32)
        group_rows.append(target_high * partner)
        if level_bit + 1 < seq_bits:
            running = running + partner
    group_sums = jnp.stack(group_rows)
    inner_rows = []
    for target in range(block_count):
        level_rows = []
        for level_bit in range(1, inner_bits):
            span = 1 << level_bit
            if target >> level_bit & 1:
                start = target >> level_bit + 1 << level_bit + 1
                total = block_states[start]
                for source in range(start + 1, start + span):
                    if source != target - 1:
                        total = total + block_states[source]
                level_rows.append(total)
            else:
                level_rows.append(jnp.zeros_like(block_states[0]))
        if level_rows:
            inner_rows.append(jnp.stack(level_rows))
    lowest_flags = jnp.stack(
        [
            ((seq_index >> level_bit & 1 == 1) & (seq_index & (1 << level_bit) - 1 == 0)).astype(
                jnp.float32
            )
            for level_bit in range(seq_bits)
        ]
    )
    first_block = (jnp.arange(block_count) == 0).astype(jnp.float32)
    correction = lowest_flags[:, None, None, None] * halo_state[None]
    outer_states = group_sums[None] - first_block[:, None, None, None, None] * correction[None]
    if inner_rows:
        inner_states = jnp.stack(inner_rows)
        outer_states = jnp.concatenate([inner_states, outer_states], 1)
    far_states = outer_states.astype(jnp.bfloat16)
    weight_blocks = jnp.transpose(
        level_weights.reshape(level_count, head_count, block_count, STRETCH), (2, 3, 1, 0)
    )
    scaled = (
        query_blocks[:, :, :, None, :] * weight_blocks[:, :, :, 2:, None] * score_scale
    ).astype(jnp.bfloat16)
    far_part = jnp.einsum(
        "cthld,clhde->cthe", scaled, far_states, preferred_element_type=jnp.float32
    )
    mixed_out = (
        weight_blocks[:, :, :, 0:1] * own_part + weight_blocks[:, :, :, 1:2] * prev_part + far_part
    )
    mixed_out = mixed_out.reshape(tok_count, head_count, head_width)
    square_sum = jnp.sum(mixed_out * mixed_out, axis=(1, 2))
    whole_sum = lax.psum(square_sum, "head")
    inverse = lax.rsqrt(whole_sum / (HEADS * HEAD_DIM) + 1e-06)
    return (mixed_out * inverse[:, None, None] * out_gain[None]).astype(jnp.bfloat16)


def solution(mesh):
    placed = (
        P("seq", "head", None),
        P("seq", "head", None),
        P("seq", "head", None),
        P(None, "head", "seq"),
        P("head", None),
    )
    return jax.shard_map(
        on_device, mesh=mesh, in_specs=placed, out_specs=P("seq", "head", None), check_vma=False
    )
```

```python
import math

import jax
import jax.numpy as jnp
import numpy as np
from jax import lax
from jax.sharding import PartitionSpec as P

HEADS = 32
HEAD_DIM = 128
STRETCH = 256


def shifted(x, axis, by):
    devices = lax.axis_size(axis)
    pairs = [(i, i + by) for i in range(devices) if 0 <= i + by < devices]
    return lax.ppermute(x, axis, pairs)


def on_device(queries, key_rows, value_rows, level_weights, out_gain):
    tok_count, head_count, head_width = queries.shape
    level_count = level_weights.shape[0]
    block_count = tok_count // STRETCH
    inner_bits = block_count.bit_length() - 1
    seq_bits = lax.axis_size("seq").bit_length() - 1
    seq_index = lax.axis_index("seq")
    score_scale = 1.0 / math.sqrt(head_width)
    query_blocks = queries.reshape(block_count, STRETCH, head_count, head_width)
    key_blocks = key_rows.reshape(block_count, STRETCH, head_count, head_width)
    value_blocks = value_rows.reshape(block_count, STRETCH, head_count, head_width)
    last_pair = jnp.stack([key_rows[tok_count - STRETCH :], value_rows[tok_count - STRETCH :]])
    arrived = shifted(last_pair, "seq", 1)
    halo_keys = arrived[0]
    halo_values = arrived[1]
    prev_keys = jnp.concatenate([halo_keys[None], key_blocks[:-1]], 0)
    prev_values = jnp.concatenate([halo_values[None], value_blocks[:-1]], 0)
    positions = jnp.arange(STRETCH)
    causal = positions[:, None] >= positions[None, :]
    own_scores = (
        jnp.einsum("cthd,cuhd->chtu", query_blocks, key_blocks, preferred_element_type=jnp.float32)
        * score_scale
    )
    own_scores = jnp.where(causal, own_scores, 0.0).astype(jnp.bfloat16)
    prev_scores = (
        jnp.einsum("cthd,cuhd->chtu", query_blocks, prev_keys, preferred_element_type=jnp.float32)
        * score_scale
    ).astype(jnp.bfloat16)
    own_part = jnp.einsum(
        "chtu,cuhd->cthd", own_scores, value_blocks, preferred_element_type=jnp.float32
    )
    prev_part = jnp.einsum(
        "chtu,cuhd->cthd", prev_scores, prev_values, preferred_element_type=jnp.float32
    )
    block_states = jnp.einsum(
        "cuhd,cuhe->chde", key_blocks, value_blocks, preferred_element_type=jnp.float32
    )
    halo_state = jnp.einsum(
        "uhd,uhe->hde", halo_keys, halo_values, preferred_element_type=jnp.float32
    )
    weight_blocks = jnp.transpose(
        level_weights.reshape(level_count, head_count, block_count, STRETCH), (2, 3, 1, 0)
    )
    scaled = (
        query_blocks[:, :, :, None, :] * weight_blocks[:, :, :, 2:, None] * score_scale
    ).astype(jnp.bfloat16)
    device_total = jnp.sum(block_states, 0).astype(jnp.bfloat16).astype(jnp.float32)
    seq_count = lax.axis_size("seq")
    group_rows = []
    running = device_total
    for level_bit in range(seq_bits):
        span = 1 << level_bit
        pairs = [(i, i ^ span) for i in range(seq_count)]
        if level_bit + 1 == seq_bits:
            pairs = [(i, i ^ span) for i in range(seq_count) if not i & span]
        partner = lax.ppermute(running.astype(jnp.bfloat16), "seq", pairs).astype(jnp.float32)
        if level_bit == min(1, seq_bits - 1):
            partner, own_part, prev_part, scaled = lax.optimization_barrier(
                (partner, own_part, prev_part, scaled)
            )
        target_high = (seq_index >> level_bit & 1 == 1).astype(jnp.float32)
        group_rows.append(target_high * partner)
        if level_bit + 1 < seq_bits:
            running = running + partner
    group_sums = jnp.stack(group_rows)
    inner_rows = []
    for target in range(block_count):
        level_rows = []
        for level_bit in range(1, inner_bits):
            span = 1 << level_bit
            if target >> level_bit & 1:
                start = target >> level_bit + 1 << level_bit + 1
                total = block_states[start]
                for source in range(start + 1, start + span):
                    if source != target - 1:
                        total = total + block_states[source]
                level_rows.append(total)
            else:
                level_rows.append(jnp.zeros_like(block_states[0]))
        if level_rows:
            inner_rows.append(jnp.stack(level_rows))
    lowest_flags = jnp.stack(
        [
            ((seq_index >> level_bit & 1 == 1) & (seq_index & (1 << level_bit) - 1 == 0)).astype(
                jnp.float32
            )
            for level_bit in range(seq_bits)
        ]
    )
    first_block = (jnp.arange(block_count) == 0).astype(jnp.float32)
    correction = lowest_flags[:, None, None, None] * halo_state[None]
    outer_states = group_sums[None] - first_block[:, None, None, None, None] * correction[None]
    if inner_rows:
        inner_states = jnp.stack(inner_rows)
        outer_states = jnp.concatenate([inner_states, outer_states], 1)
    far_states = outer_states.astype(jnp.bfloat16)
    far_part = jnp.einsum(
        "cthld,clhde->cthe", scaled, far_states, preferred_element_type=jnp.float32
    )
    mixed_out = (
        weight_blocks[:, :, :, 0:1] * own_part + weight_blocks[:, :, :, 1:2] * prev_part + far_part
    )
    mixed_out = mixed_out.reshape(tok_count, head_count, head_width)
    square_sum = jnp.sum(mixed_out * mixed_out, axis=(1, 2))
    whole_sum = lax.psum(square_sum, "head")
    inverse = lax.rsqrt(whole_sum / (HEADS * HEAD_DIM) + 1e-06)
    return (mixed_out * inverse[:, None, None] * out_gain[None]).astype(jnp.bfloat16)


def solution(mesh):
    placed = (
        P("seq", "head", None),
        P("seq", "head", None),
        P("seq", "head", None),
        P(None, "head", "seq"),
        P("head", None),
    )
    return jax.shard_map(
        on_device, mesh=mesh, in_specs=placed, out_specs=P("seq", "head", None), check_vma=False
    )
```

```python
import math

import jax
import jax.numpy as jnp
import numpy as np
from jax import lax
from jax.sharding import PartitionSpec as P

HEADS = 32
HEAD_DIM = 128
STRETCH = 256


def shifted(x, axis, by):
    devices = lax.axis_size(axis)
    pairs = [(i, i + by) for i in range(devices) if 0 <= i + by < devices]
    return lax.ppermute(x, axis, pairs)


def on_device(queries, key_rows, value_rows, level_weights, out_gain):
    tok_count, head_count, head_width = queries.shape
    level_count = level_weights.shape[0]
    block_count = tok_count // STRETCH
    inner_bits = block_count.bit_length() - 1
    seq_bits = lax.axis_size("seq").bit_length() - 1
    seq_index = lax.axis_index("seq")
    score_scale = 1.0 / math.sqrt(head_width)
    query_blocks = queries.reshape(block_count, STRETCH, head_count, head_width)
    key_blocks = key_rows.reshape(block_count, STRETCH, head_count, head_width)
    value_blocks = value_rows.reshape(block_count, STRETCH, head_count, head_width)
    last_pair = jnp.stack([key_rows[tok_count - STRETCH :], value_rows[tok_count - STRETCH :]])
    arrived = shifted(last_pair, "seq", 1)
    halo_keys = arrived[0]
    halo_values = arrived[1]
    positions = jnp.arange(STRETCH)
    causal = positions[:, None] >= positions[None, :]
    own_scores = (
        jnp.einsum("cthd,cuhd->chtu", query_blocks, key_blocks, preferred_element_type=jnp.float32)
        * score_scale
    )
    own_scores = jnp.where(causal, own_scores, 0.0).astype(jnp.bfloat16)
    prev_scores = (
        jnp.concatenate(
            [
                jnp.einsum(
                    "thd,uhd->htu", query_blocks[0], halo_keys, preferred_element_type=jnp.float32
                )[None],
                jnp.einsum(
                    "cthd,cuhd->chtu",
                    query_blocks[1:],
                    key_blocks[:-1],
                    preferred_element_type=jnp.float32,
                ),
            ],
            0,
        )
        * score_scale
    ).astype(jnp.bfloat16)
    own_part = jnp.einsum(
        "chtu,cuhd->cthd", own_scores, value_blocks, preferred_element_type=jnp.float32
    )
    prev_part = jnp.concatenate(
        [
            jnp.einsum(
                "htu,uhd->thd", prev_scores[0], halo_values, preferred_element_type=jnp.float32
            )[None],
            jnp.einsum(
                "chtu,cuhd->cthd", prev_scores[1:], value_blocks[:-1], preferred_element_type=jnp.float32
            ),
        ],
        0,
    )
    block_states = jnp.einsum(
        "cuhd,cuhe->chde", key_blocks, value_blocks, preferred_element_type=jnp.float32
    )
    halo_state = jnp.einsum(
        "uhd,uhe->hde", halo_keys, halo_values, preferred_element_type=jnp.float32
    )
    weight_blocks = jnp.transpose(
        level_weights.reshape(level_count, head_count, block_count, STRETCH), (2, 3, 1, 0)
    )
    scaled = (
        query_blocks[:, :, :, None, :] * weight_blocks[:, :, :, 2:, None] * score_scale
    ).astype(jnp.bfloat16)
    device_total = jnp.sum(block_states, 0).astype(jnp.bfloat16).astype(jnp.float32)
    seq_count = lax.axis_size("seq")
    group_rows = []
    running = device_total
    for level_bit in range(seq_bits):
        span = 1 << level_bit
        pairs = [(i, i ^ span) for i in range(seq_count)]
        if level_bit + 1 == seq_bits:
            pairs = [(i, i ^ span) for i in range(seq_count) if not i & span]
        partner = lax.ppermute(running.astype(jnp.bfloat16), "seq", pairs).astype(jnp.float32)
        if level_bit == min(1, seq_bits - 1):
            partner, own_part, prev_part, scaled = lax.optimization_barrier(
                (partner, own_part, prev_part, scaled)
            )
        target_high = (seq_index >> level_bit & 1 == 1).astype(jnp.float32)
        group_rows.append(target_high * partner)
        if level_bit + 1 < seq_bits:
            running = running + partner
    group_sums = jnp.stack(group_rows)
    inner_rows = []
    for target in range(block_count):
        level_rows = []
        for level_bit in range(1, inner_bits):
            span = 1 << level_bit
            if target >> level_bit & 1:
                start = target >> level_bit + 1 << level_bit + 1
                total = block_states[start]
                for source in range(start + 1, start + span):
                    if source != target - 1:
                        total = total + block_states[source]
                level_rows.append(total)
            else:
                level_rows.append(jnp.zeros_like(block_states[0]))
        if level_rows:
            inner_rows.append(jnp.stack(level_rows))
    lowest_flags = jnp.stack(
        [
            ((seq_index >> level_bit & 1 == 1) & (seq_index & (1 << level_bit) - 1 == 0)).astype(
                jnp.float32
            )
            for level_bit in range(seq_bits)
        ]
    )
    first_block = (jnp.arange(block_count) == 0).astype(jnp.float32)
    correction = lowest_flags[:, None, None, None] * halo_state[None]
    outer_states = group_sums[None] - first_block[:, None, None, None, None] * correction[None]
    if inner_rows:
        inner_states = jnp.stack(inner_rows)
        outer_states = jnp.concatenate([inner_states, outer_states], 1)
    far_states = outer_states.astype(jnp.bfloat16)
    far_part = jnp.einsum(
        "cthld,clhde->cthe", scaled, far_states, preferred_element_type=jnp.float32
    )
    mixed_out = (
        weight_blocks[:, :, :, 0:1] * own_part + weight_blocks[:, :, :, 1:2] * prev_part + far_part
    )
    mixed_out = mixed_out.reshape(tok_count, head_count, head_width)
    square_sum = jnp.sum(mixed_out * mixed_out, axis=(1, 2))
    whole_sum = lax.psum(square_sum, "head")
    inverse = lax.rsqrt(whole_sum / (HEADS * HEAD_DIM) + 1e-06)
    return (mixed_out * inverse[:, None, None] * out_gain[None]).astype(jnp.bfloat16)


def solution(mesh):
    placed = (
        P("seq", "head", None),
        P("seq", "head", None),
        P("seq", "head", None),
        P(None, "head", "seq"),
        P("head", None),
    )
    return jax.shard_map(
        on_device, mesh=mesh, in_specs=placed, out_specs=P("seq", "head", None), check_vma=False
    )
```
